512 devices in a mesh: req: 32 (over z, core), mlp: 16 (over y, x).
Axes of the slice: x: 4, y: 4, z: 16, core: 2. Of those that a mesh axis runs over, the one named last changes fastest.
Arguments:
- hidden_input: bfloat16 [12288, 4096], P('req', 'mlp'), may hold values from -6 to 6
- input_norm_gain: bfloat16 [4096], replicated, may hold values from 0.099609375 to 1.8984375
- query_norm_gain: bfloat16 [128], replicated, may hold values from 0.099609375 to 1.8984375
- key_norm_gain: bfloat16 [128], replicated, may hold values from 0.099609375 to 1.8984375
- query_weight: bfloat16 [4096, 4096], P('req', 'mlp'), may hold values from -0.09375 to 0.09375
- key_value_weight: bfloat16 [4096, 2, 1024], P('req'), may hold values from -0.09375 to 0.09375
- output_weight: bfloat16 [4096, 16, 256], P('mlp', None, 'req'), may hold values from -0.09375 to 0.09375
- adapter_down_qkv: bfloat16 [64, 48, 4096], P('req', None, 'mlp'), may hold values from -0.09375 to 0.09375
- adapter_down_output: bfloat16 [64, 16, 4096], P('req', None, 'mlp'), may hold values from -0.09375 to 0.09375
- adapter_up_query: bfloat16 [64, 16, 4096], P('req', None, 'mlp'), may hold values from -1.5 to 1.5
- adapter_up_key_value: bfloat16 [64, 16, 2, 1024], P('req'), may hold values from -1.5 to 1.5
- adapter_up_output: bfloat16 [64, 16, 4096], P('req', None, 'mlp'), may hold values from -1.5 to 1.5
- pool: bfloat16 [16384, 2, 1024], P('req'), may hold values from -6 to 6
- lengths: int32 [32, 4], P('req'), may hold values from 1 to 192, 384 in all within a row
- cached_prefix_pages: int32 [32, 4], P('req'), may hold values from 0 to 8
- prefix_page_table: int32 [32, 4, 8], P('req'), may hold values from 0 to 7, each once within a row
- adapter_of_request: int32 [32, 4, 1], P('req'), may hold values from 0 to 63
- adapter_storage: int32 [64], replicated, may hold values from 0 to 63, each once
Outputs:
- attention_update: bfloat16 [12288, 4096], P('req', 'mlp')
- new_cache: bfloat16 [12288, 2, 1024], P('req', None, 'mlp')
The draws below stay inside these ranges and needn't reach their ends.
Inputs may be any that keep to these rules, and one draw needn't show every extreme that they name: The lengths of one index of req sum to 384, and the longest of them is 192. `prefix_page_table`: each row lists every page of its pool once. `adapter_of_request`: every adapter is used by some request. `adapter_storage`: each slot holds one adapter.
All inputs are finite; a program needn't handle non-finite values.
Results may differ from the reference program's by a relative error of at most 0.035.
Values may be sent and summed in bfloat16 or wider, within the bound.
A program may use at most 64 MiB of HBM per device.

```python
import math
import jax
import jax.numpy as jnp
import numpy as np
from jax import lax

MODEL_WIDTH = 4096
QUERY_HEADS = 32
KEY_VALUE_HEADS = 8
HEAD_SIZE = 128
ADAPTER_RANK = 16
REQ_GRP = 4
GROUP_TOKENS = 384
PAGE = 64
POOL_PAGES = 8
ADAPTER_COUNT = 64
TOKENS = 12288
CACHED_TOKENS = 16384
N_REQ = 32
N_MLP = 16


def with_ends(drawn, rng, low, high):
    spot = [jax.random.randint(jax.random.fold_in(rng, axis), (), 0, length) for axis, length in enumerate(drawn.shape)]
    main_axis = drawn.shape.index(max(drawn.shape))
    next_to = spot[:main_axis] + [(spot[main_axis] + 1) % drawn.shape[main_axis]] + spot[main_axis + 1:]
    return drawn.at[tuple(spot)].set(low).at[tuple(next_to)].set(high)


def shard_levels(own_key, extent, pieces, low, top_value):
    loudness = 1.0
    for position, blocks in pieces:
        steps = jax.random.uniform(jax.random.fold_in(jax.random.fold_in(own_key, 6), position), (blocks,), jnp.float32, low / len(pieces), top_value / len(pieces))
        loudness = loudness * jnp.repeat(jnp.exp(steps), extent[position] // blocks).reshape((-1,) + (1,) * (len(extent) - 1 - position))
    return loudness


def different_ones(own_key, rows, amount, top, lift):
    order = jax.random.permutation(jax.random.fold_in(own_key, 1), amount)
    pull = order
    for power in range(3):
        pull = pull * pull // amount
    pull = pull * lift // amount
    lots = jax.random.randint(jax.random.fold_in(own_key, 2), (rows, amount), 0, 4096) + pull
    fixed_rows = jax.random.permutation(jax.random.fold_in(own_key, 3), rows)[jnp.arange(amount) % rows]
    lots = jnp.where(jnp.arange(rows)[:, None] == fixed_rows[None, :], 1 << 14, lots)
    priority = lots * amount + jnp.arange(amount)
    return lax.top_k(priority.astype(jnp.int32), top)[1].astype(jnp.int32)


def length_profile(amount, total, reach, skew):
    portions = [(1 << 20) // math.isqrt(grade ** skew) + 1 for grade in range(2, amount + 1)]
    surplus, holding = total - reach - (amount - 1), [1] * (amount - 1)
    while surplus > 0:
        candidates = [i for i in range(amount - 1) if holding[i] < reach]
        whole, remaining = sum([portions[i] for i in candidates]), surplus
        for i in candidates:
            extra = min(reach - holding[i], max(1, remaining * portions[i] // whole), surplus)
            holding[i] = holding[i] + extra
            surplus = surplus - extra
    return np.array([reach] + holding)


def uneven(stream_key, number_of, total, reach, lean):
    if number_of == 2:
        one = jax.random.randint(stream_key, (), max(1, total - reach), min(reach, total - 1) + 1)
        return jnp.stack([one, total - one])
    tallies = jnp.asarray(length_profile(number_of, total, reach, lean), jnp.int32)
    pairs = (number_of - 1) // 2
    donor, receiver = tallies[1:1 + 2 * pairs:2], tallies[2:2 + 2 * pairs:2]
    margin = jnp.minimum(donor - 1, reach - receiver)
    passed = jax.random.randint(jax.random.fold_in(stream_key, 1), (pairs,), 0, 1 << 20) % (margin + 1)
    tallies = tallies.at[1:1 + 2 * pairs:2].set(donor - passed).at[2:2 + 2 * pairs:2].set(receiver + passed)
    return tallies[jax.random.permutation(jax.random.fold_in(stream_key, 2), number_of)]


def centred(own_key, extent, deviation, most, split=(), kind=jnp.bfloat16):
    entries = jax.random.normal(own_key, extent, jnp.float32) * deviation
    if len(split) > 0:
        entries = shard_levels(own_key, extent, split, -0.22, 0.18) * entries
    return jnp.clip(entries, min=-most, max=most).astype(kind)


def setup_inputs(seed: int = 0) -> dict:
    seeds = jax.random.split(jax.random.key(seed), 19)
    return {
        "hidden_input": centred(seeds[0], (TOKENS, MODEL_WIDTH), 1.0, 6.0, ((0, 32), (1, 16))),
        "input_norm_gain": jnp.clip(1.0 + 0.18 * jax.random.normal(seeds[1], (MODEL_WIDTH,), jnp.float32), 0.099609375, 1.8984375).astype(jnp.bfloat16),
        "query_norm_gain": jnp.clip(1.0 + 0.18 * jax.random.normal(seeds[2], (HEAD_SIZE,), jnp.float32), 0.099609375, 1.8984375).astype(jnp.bfloat16),
        "key_norm_gain": jnp.clip(1.0 + 0.18 * jax.random.normal(seeds[3], (HEAD_SIZE,), jnp.float32), 0.099609375, 1.8984375).astype(jnp.bfloat16),
        "query_weight": centred(seeds[4], (MODEL_WIDTH, QUERY_HEADS * HEAD_SIZE), MODEL_WIDTH ** -0.5, 0.09375, ((0, 32), (1, 16))),
        "key_value_weight": centred(seeds[5], (MODEL_WIDTH, 2, KEY_VALUE_HEADS * HEAD_SIZE), MODEL_WIDTH ** -0.5, 0.09375, ((0, 32),)),
        "output_weight": centred(seeds[6], (QUERY_HEADS * HEAD_SIZE, N_MLP, MODEL_WIDTH // N_MLP), (QUERY_HEADS * HEAD_SIZE) ** -0.5, 0.09375, ((0, 16), (2, 32))),
        "adapter_down_qkv": centred(seeds[7], (ADAPTER_COUNT, 3 * ADAPTER_RANK, MODEL_WIDTH), MODEL_WIDTH ** -0.5, 0.09375, ((0, 32), (2, 16))),
        "adapter_down_output": centred(seeds[8], (ADAPTER_COUNT, ADAPTER_RANK, QUERY_HEADS * HEAD_SIZE), (QUERY_HEADS * HEAD_SIZE) ** -0.5, 0.09375, ((0, 32), (2, 16))),
        "adapter_up_query": centred(seeds[9], (ADAPTER_COUNT, ADAPTER_RANK, QUERY_HEADS * HEAD_SIZE), ADAPTER_RANK ** -0.5, 1.5, ((0, 32), (2, 16))),
        "adapter_up_key_value": centred(seeds[10], (ADAPTER_COUNT, ADAPTER_RANK, 2, KEY_VALUE_HEADS * HEAD_SIZE), ADAPTER_RANK ** -0.5, 1.5, ((0, 32),)),
        "adapter_up_output": centred(seeds[11], (ADAPTER_COUNT, ADAPTER_RANK, MODEL_WIDTH), ADAPTER_RANK ** -0.5, 1.5, ((0, 32), (2, 16))),
        "pool": centred(seeds[12], (CACHED_TOKENS, 2, KEY_VALUE_HEADS * HEAD_SIZE), 1.0, 6.0, ((0, 32),)),
        "lengths": jax.vmap(lambda own: uneven(own, REQ_GRP, GROUP_TOKENS, GROUP_TOKENS // 2, 2))(jax.random.split(seeds[13], N_REQ)).reshape((N_REQ, REQ_GRP)).astype(jnp.int32),
        "cached_prefix_pages": with_ends(jax.random.randint(seeds[14], (N_REQ, REQ_GRP), 0, POOL_PAGES + 1), jax.random.fold_in(seeds[14], 1), 0, POOL_PAGES).astype(jnp.int32),
        "prefix_page_table": jax.vmap(lambda own: jax.random.permutation(own, POOL_PAGES))(jax.random.split(seeds[15], N_REQ * REQ_GRP)).reshape((N_REQ, REQ_GRP, POOL_PAGES)).astype(jnp.int32),
        "adapter_of_request": different_ones(seeds[16], N_REQ * REQ_GRP, ADAPTER_COUNT, 1, 128).reshape((N_REQ, REQ_GRP, 1)),
        "adapter_storage": jax.random.permutation(seeds[17], ADAPTER_COUNT).astype(jnp.int32),
    }


epsilon = 1e-06
rope_base = 1000000.0

def root_mean_scale(values, gain_vec):
    mean_sq = lax.optimization_barrier(jnp.mean(values * values, axis=-1, keepdims=True))
    return values * lax.rsqrt(mean_sq + epsilon) * gain_vec.astype(jnp.float32)

def rotary_embed(values, token_positions):
    half_width = values.shape[-1] // 2
    inverse_freq = jnp.exp(jnp.arange(half_width, dtype=jnp.float32) * (-2.0 / values.shape[-1]) * math.log(rope_base))
    angles = token_positions.astype(jnp.float32)[:, None] * inverse_freq[None, :]
    cosine = jnp.cos(angles)[:, None, :]
    sine_part = jnp.sin(angles)[:, None, :]
    front = values[..., :half_width]
    back = values[..., half_width:]
    return jnp.concatenate([front * cosine - back * sine_part, back * cosine + front * sine_part], axis=-1)

def row_tables(lengths_row, prefix_row, page_rows, row_count):
    ends_at = jnp.cumsum(lengths_row).astype(jnp.int32)
    starts_at = (ends_at - lengths_row).astype(jnp.int32)
    row_ids = jnp.arange(row_count, dtype=jnp.int32)
    owners = lax.optimization_barrier(jnp.sum((row_ids[:, None] >= ends_at[None, :]).astype(jnp.int32), axis=1)).astype(jnp.int32)
    group_members = owners[:, None] == jnp.arange(lengths_row.shape[0], dtype=jnp.int32)[None, :]
    offsets = PAGE * prefix_row[None, :] + row_ids[:, None] - starts_at[None, :]
    token_positions = lax.optimization_barrier(jnp.sum(jnp.where(group_members, offsets, 0), axis=1)).astype(jnp.int32)
    page_ids = jnp.arange(page_rows.shape[1], dtype=jnp.int32)
    listed = (page_rows[:, :, None] == page_ids[None, None, :]) & (page_ids[None, :, None] < prefix_row[:, None, None])
    page_used = lax.optimization_barrier(jnp.sum(listed.astype(jnp.float32), axis=1))
    return (owners, group_members, token_positions, page_used)

def apply_adapter(lowrank_inner, group_members, chosen_up):
    masked = lowrank_inner.astype(jnp.float32)[:, None, :] * group_members.astype(jnp.float32)[:, :, None]
    return jnp.einsum('gjr,jrc->gc', masked, chosen_up.astype(jnp.float32))

def reference(hidden_input, input_norm_gain, query_norm_gain, key_norm_gain, query_weight, key_value_weight, output_weight, adapter_down_qkv, adapter_down_output, adapter_up_query, adapter_up_key_value, adapter_up_output, pool, lengths, cached_prefix_pages, prefix_page_table, adapter_of_request, adapter_storage):
    key_value_width = KEY_VALUE_HEADS * HEAD_SIZE
    block_rows = QUERY_HEADS * HEAD_SIZE // N_MLP
    w_blocks = output_weight.reshape(QUERY_HEADS * HEAD_SIZE, MODEL_WIDTH).astype(jnp.float32).reshape(N_MLP, block_rows, MODEL_WIDTH)
    pool_token_rows = POOL_PAGES * PAGE

    def one_group(inputs_group):
        tokens, lengths_row, prefix_row, page_rows, chosen, pool_index_group = inputs_group
        owners, group_members, token_positions, page_used = row_tables(lengths_row, prefix_row, page_rows, GROUP_TOKENS)
        slot_indices = jnp.take(adapter_storage, chosen, axis=0)
        normalized_input = root_mean_scale(tokens.astype(jnp.float32), input_norm_gain).astype(jnp.bfloat16)
        chosen_down = jnp.take(adapter_down_qkv, slot_indices, axis=0).astype(jnp.float32)
        low_terms = jnp.einsum('gd,jkd->gjk', normalized_input.astype(jnp.float32), chosen_down)
        lowrank_inner = lax.optimization_barrier(jnp.sum(low_terms * group_members.astype(jnp.float32)[:, :, None], axis=1)).astype(jnp.bfloat16)
        query_plain = (jnp.dot(normalized_input, query_weight, preferred_element_type=jnp.float32) + apply_adapter(lowrank_inner[:, 0:ADAPTER_RANK], group_members, jnp.take(adapter_up_query, slot_indices, axis=0))).astype(jnp.bfloat16)
        key_value_chosen = jnp.take(adapter_up_key_value, slot_indices, axis=0)
        kv_base = jnp.dot(normalized_input, key_value_weight.reshape(MODEL_WIDTH, 2 * key_value_width), preferred_element_type=jnp.float32).reshape(GROUP_TOKENS, 2, key_value_width)
        key_lowrank_part = apply_adapter(lowrank_inner[:, ADAPTER_RANK:2 * ADAPTER_RANK], group_members, key_value_chosen[:, :, 0])
        value_lowrank_part = apply_adapter(lowrank_inner[:, 2 * ADAPTER_RANK:3 * ADAPTER_RANK], group_members, key_value_chosen[:, :, 1])
        key_value_plain = (kv_base + jnp.stack([key_lowrank_part, value_lowrank_part], axis=1)).astype(jnp.bfloat16)
        query_rotated = rotary_embed(root_mean_scale(query_plain.astype(jnp.float32).reshape(GROUP_TOKENS, QUERY_HEADS, HEAD_SIZE), query_norm_gain), token_positions).astype(jnp.bfloat16)
        key_rotated = rotary_embed(root_mean_scale(key_value_plain[:, 0].astype(jnp.float32).reshape(GROUP_TOKENS, KEY_VALUE_HEADS, HEAD_SIZE), key_norm_gain), token_positions).astype(jnp.bfloat16)
        cache_group = jnp.stack([key_rotated.reshape(GROUP_TOKENS, key_value_width), key_value_plain[:, 1]], axis=1)
        key_matrix = jnp.concatenate([pool_index_group[:, 0].reshape(pool_token_rows, KEY_VALUE_HEADS, HEAD_SIZE), key_rotated], axis=0)
        value_matrix = jnp.concatenate([pool_index_group[:, 1].reshape(pool_token_rows, KEY_VALUE_HEADS, HEAD_SIZE), key_value_plain[:, 1].reshape(GROUP_TOKENS, KEY_VALUE_HEADS, HEAD_SIZE)], axis=0)
        pool_ok = jnp.dot(group_members.astype(jnp.float32), page_used, precision=lax.Precision.HIGHEST)
        pool_ok = jnp.repeat(pool_ok, PAGE, axis=1) > 0.5
        row_ids = jnp.arange(GROUP_TOKENS, dtype=jnp.int32)
        causal = (owners[:, None] == owners[None, :]) & (row_ids[None, :] <= row_ids[:, None])
        allowed = jnp.concatenate([pool_ok, causal], axis=1)
        query_rows = query_rotated.astype(jnp.float32).reshape(GROUP_TOKENS, KEY_VALUE_HEADS, QUERY_HEADS // KEY_VALUE_HEADS, HEAD_SIZE)
        scores = jnp.einsum('gkhd,skd->khgs', query_rows, key_matrix.astype(jnp.float32)) / math.sqrt(HEAD_SIZE)
        exp_scores = jnp.where(allowed[None, None], jnp.exp(scores), 0.0)
        softmax = (exp_scores / lax.optimization_barrier(jnp.sum(exp_scores, axis=-1, keepdims=True))).astype(jnp.bfloat16)
        attended = jnp.einsum('khgs,skd->gkhd', softmax.astype(jnp.float32), value_matrix.astype(jnp.float32))
        attended = attended.astype(jnp.bfloat16).reshape(GROUP_TOKENS, QUERY_HEADS * HEAD_SIZE)
        output_down = jnp.take(adapter_down_output, slot_indices, axis=0).astype(jnp.float32)
        out_terms = jnp.einsum('gc,jrc->gjr', attended.astype(jnp.float32), output_down)
        lowrank_result = lax.optimization_barrier(jnp.sum(out_terms * group_members.astype(jnp.float32)[:, :, None], axis=1)).astype(jnp.bfloat16)
        parts = jnp.einsum('gmc,mcd->gmd', attended.astype(jnp.float32).reshape(GROUP_TOKENS, N_MLP, block_rows), w_blocks)
        parts = lax.optimization_barrier(parts.astype(jnp.bfloat16))
        head_count_all = lax.optimization_barrier(jnp.sum(parts.astype(jnp.float32), axis=1))
        output_update = (head_count_all + apply_adapter(lowrank_result, group_members, jnp.take(adapter_up_output, slot_indices, axis=0))).astype(jnp.bfloat16)
        return (output_update, cache_group)
    output_update, cache_all = lax.map(one_group, (hidden_input.reshape(N_REQ, GROUP_TOKENS, MODEL_WIDTH), lengths, cached_prefix_pages, prefix_page_table, adapter_of_request[:, :, 0], pool.reshape(N_REQ, pool_token_rows, 2, key_value_width)))
    return (output_update.reshape(TOKENS, MODEL_WIDTH), cache_all.reshape(TOKENS, 2, key_value_width))
```

```python
import functools
import math

import jax
import jax.numpy as jnp
from jax import lax
from jax.experimental import pallas as pl
from jax.experimental.pallas import tpu as pltpu
from jax.sharding import PartitionSpec as P

QUERY_HEADS = 32
KEY_VALUE_HEADS = 8
HEAD_SIZE = 128
ADAPTER_RANK = 16
PAGE = 64
MESH = pl.DeviceIdType.MESH

epsilon = 1e-06
rope_base = 1000000.0

Z_COUNT, NX, NY = 16, 4, 4
ROWS, COLS = 384, 256


class Links:
    def __init__(self, send, recv):
        self.send, self.recv, self.used, self.pending = send, recv, 0, []

    def start(self, src, dst, device):
        slot = self.used
        self.used += 1
        copy = pltpu.make_async_remote_copy(
            src_ref=src,
            dst_ref=dst,
            send_sem=self.send.at[slot],
            recv_sem=self.recv.at[slot],
            device_id=device,
            device_id_type=MESH,
        )
        copy.start()
        self.pending.append(copy)
        return copy

    def drain(self):
        for copy in self.pending:
            copy.wait_send()
        self.pending = []


class Place:
    def __init__(self):
        self.r = lax.axis_index("req")
        self.m = lax.axis_index("mlp")
        self.x = lax.rem(self.m, NX)
        self.y = lax.div(self.m, NX)

    def along(self, axis, step):
        if axis == "x":
            return self.m - self.x + lax.rem(self.x + (step + NX), NX)
        return lax.rem(self.m + (step + NY) * NX, NX * NY)

    def at(self, axis_a, i, axis_b, j):
        x = self.x + (i if axis_a == "x" else j) + NX
        y = self.y + (i if axis_a == "y" else j) + NY
        return lax.rem(y, NY) * NX + lax.rem(x, NX)


def barrier(place, whole_plane):
    sem = pltpu.get_barrier_semaphore()
    n = 0
    r, m = place.r, place.m
    for other in (lax.rem(r + 2, 32), lax.rem(r + 30, 32), r + 1 - 2 * lax.rem(r, 2)):
        pl.semaphore_signal(sem, inc=1, device_id=(other, m), device_id_type=MESH)
        n += 1
    for d in range(1, NX * NY):
        other = lax.rem(m + d, NX * NY)
        pl.semaphore_signal(sem, inc=1, device_id=(r, other), device_id_type=MESH)
        n += 1
    pl.semaphore_wait(sem, n)


class PlaneGather:
    def __init__(self, links, place, buf, rows):
        self.links, self.place, self.buf, self.rows = links, place, buf, rows
        self.p1, self.p2, self.q1, self.q2 = {}, {}, {}, {}
        self.axes = [("x", "y"), ("y", "x")]

    def view(self, h, piece, part=None):
        rows = self.rows // 2
        begin = h * rows
        if part is not None:
            rows //= 2
            begin += part * rows
        return self.buf.at[piece, pl.ds(begin, rows), :]

    def send(self, h, axis, step, piece, part=None):
        view = self.view(h, piece, part)
        return self.links.start(view, view, (self.place.r, self.place.along(axis, step)))

    def piece(self, h, i):
        a, b = self.axes[h]
        return self.place.at(a, i, b, 0)

    def start_second(self, h, i):
        b = self.axes[h][1]
        for s in (1, -1):
            self.q1[h, i, s] = self.send(h, b, s, self.piece(h, i))

    def e0(self):
        for h in range(2):
            a = self.axes[h][0]
            for s in (1, -1):
                self.p1[h, s] = self.send(h, a, s, self.place.m)
        for h in range(2):
            self.start_second(h, 0)

    def e1(self):
        for h in range(2):
            a = self.axes[h][0]
            for s in (1, -1):
                self.p1[h, s].wait_recv()
                self.p2[h, s] = self.send(h, a, s, self.piece(h, -s), 0 if s == 1 else 1)
        for h in range(2):
            for s in (1, -1):
                self.start_second(h, -s)

    def e2(self):
        for h in range(2):
            for s in (1, -1):
                self.p2[h, s].wait_recv()
            self.start_second(h, 2)

    def e3(self, i):
        for h in range(2):
            a, b = self.axes[h]
            for s in (1, -1):
                self.q1[h, i, s].wait_recv()
                piece = self.place.at(a, i, b, -s)
                self.q2[h, i, s] = self.send(h, b, s, piece, 0 if s == 1 else 1)

    def e4(self):
        for copy in self.q2.values():
            copy.wait_recv()

    def run(self):
        self.e0()
        self.e1()
        self.e2()
        for i in (0, -1, 1, 2):
            self.e3(i)
        self.e4()


class RingGather:
    def __init__(self, links, place, view, halves):
        self.links, self.place, self.view, self.halves = links, place, view, halves
        self.z, self.sib = {}, []

    def shard(self, t):
        return lax.rem(self.place.r + (2 * t + 32), 32)

    def send(self, t, s):
        shard = self.shard(-s * t)
        target = (lax.rem(self.place.r + (2 * s + 32), 32), self.place.m)
        if t == Z_COUNT // 2 - 1:
            view = self.halves(shard, 0 if s == 1 else 1)
        else:
            view = self.view(shard)
        self.z[t, s] = self.links.start(view, view, target)

    def sibling(self, t):
        view = self.view(self.shard(t))
        r = self.place.r
        self.sib.append(
            self.links.start(view, view, (r + 1 - 2 * lax.rem(r, 2), self.place.m))
        )

    def step(self, t):
        last = Z_COUNT // 2
        if t == 0:
            for s in (1, -1):
                self.send(0, s)
            self.sibling(0)
            return
        for s in (1, -1):
            self.z[t - 1, s].wait_recv()
            if t < last:
                self.send(t, s)
        if t < last:
            for s in (1, -1):
                self.sibling(-s * t)
        else:
            self.sibling(last)

    def finish(self):
        for copy in self.sib:
            copy.wait_recv()


def halves_of(ref, rows):
    return (
        lambda shard: ref.at[shard],
        lambda shard, part: ref.at[shard, pl.ds(part * (rows // 2), rows // 2), :],
    )


def gather_kernel(
    lengths,
    chosen,
    storage,
    hid,
    gain,
    down_qkv,
    wq,
    wkv,
    up_q,
    up_kv,
    down_out,
    up_out,
    wo,
    hid_all,
    mid_all,
    late_all,
    wo_all,
    low_out,
    down_all,
    low_all,
    send,
    recv,
    local,
):
    place = Place()
    r, m = place.r, place.m
    links = Links(send, recv)

    staged = []

    def stage(src, dst):
        copy = pltpu.make_async_copy(src, dst, local.at[len(staged)])
        copy.start()
        staged.append(copy)

    for i in range(2):
        stage(down_qkv.at[i], down_all.at[r, pl.ds(48 * i, 48), :])
    stage(hid, hid_all.at[m])
    stage(wq, mid_all.at[r, pl.ds(0, 128), :])
    stage(wkv, mid_all.at[r, pl.ds(128, 128), :])
    for i in range(2):
        stage(up_q.at[i], mid_all.at[r, pl.ds(256 + 16 * i, 16), :])
        stage(up_kv.at[i], mid_all.at[r, pl.ds(288 + 16 * i, 16), :])
        stage(down_out.at[i], late_all.at[r, pl.ds(16 * i, 16), :])
        stage(up_out.at[i], late_all.at[r, pl.ds(32 + 16 * i, 16), :])
    stage(wo.at[m], wo_all.at[m, pl.ds(r * 8, 8), :])
    barrier(place, True)
    for copy in staged:
        copy.wait()

    plane = PlaneGather(links, place, hid_all, ROWS)
    early = RingGather(links, place, *halves_of(down_all, 96))
    mid = RingGather(links, place, *halves_of(mid_all, 320))
    late = RingGather(links, place, *halves_of(late_all, 64))
    out = RingGather(
        links,
        place,
        lambda shard: wo_all.at[:, pl.ds(shard * 8, 8), :],
        lambda shard, part: wo_all.at[pl.ds(8 * part, 8), pl.ds(shard * 8, 8), :],
    )

    early.step(0)
    plane.e0()
    mid.step(0)
    swaps = []
    for d in range(1, 16):
        other = lax.rem(m + d, 16)
        swaps.append(links.start(wo.at[other], wo_all.at[m, pl.ds(r * 8, 8), :], (r, other)))
    early.step(1)
    plane.e1()
    mid.step(1)
    early.step(2)
    plane.e2()
    mid.step(2)
    for copy in swaps:
        copy.wait_recv()
    early.step(3)
    plane.e3(0)
    mid.step(3)
    early.step(4)
    late.step(0)
    out.step(0)
    plane.e3(-1)
    mid.step(4)
    early.step(5)
    plane.e3(1)
    mid.step(5)
    early.step(6)
    plane.e3(2)
    mid.step(6)
    early.step(7)
    mid.step(7)
    early.step(8)
    early.finish()

    e1 = lengths[0, 0]
    e2 = e1 + lengths[0, 1]
    e3 = e2 + lengths[0, 2]
    token = lax.broadcasted_iota(jnp.int32, (1, ROWS), 1)
    owner = (
        (token >= e1).astype(jnp.int32)
        + (token >= e2).astype(jnp.int32)
        + (token >= e3).astype(jnp.int32)
    )
    scaled = (hid[...].astype(jnp.float32) * gain[...]).astype(jnp.bfloat16)
    low = jnp.zeros((48, ROWS), jnp.float32)
    for j in range(4):
        slot = storage[chosen[0, j]]
        down = down_all[slot // 2, pl.ds((slot % 2) * 48, 48), :]
        terms = lax.dot_general(
            down, scaled, (((1,), (1,)), ((), ())), preferred_element_type=jnp.float32
        )
        low = low + jnp.where(owner == j, terms, 0.0)
    low_all[m, 0:48, :] = low.astype(jnp.bfloat16)
    low_all[m, 48:64, :] = jnp.zeros((16, ROWS), jnp.bfloat16)
    lows = PlaneGather(links, place, low_all, 64)
    lows.e0()
    mid.step(8)
    lows.e1()
    late.step(1)
    out.step(1)
    lows.e2()
    late.step(2)
    out.step(2)
    for i in (0, -1, 1, 2):
        lows.e3(i)
    for t in range(3, 9):
        late.step(t)
        out.step(t)
    lows.e4()
    total = jnp.zeros((64, ROWS), jnp.float32)
    for i in range(16):
        total = total + low_all[i].astype(jnp.float32)
    low_out[...] = total
    plane.e4()
    mid.finish()
    late.finish()
    out.finish()
    links.drain()


def gather_attended_kernel(att, low, att_all, low_all, send, recv, local):
    place = Place()
    links = Links(send, recv)
    a = pltpu.make_async_copy(att, att_all.at[place.m], local.at[0])
    b = pltpu.make_async_copy(low, low_all.at[place.m], local.at[1])
    a.start()
    b.start()
    barrier(place, False)
    a.wait()
    b.wait()
    plane = PlaneGather(links, place, att_all, ROWS)
    lows = PlaneGather(links, place, low_all, 32)
    lows.e0()
    plane.e0()
    lows.e1()
    plane.e1()
    lows.e2()
    plane.e2()
    for i in (0, -1, 1, 2):
        lows.e3(i)
        plane.e3(i)
    lows.e4()
    plane.e4()
    links.drain()


def rotary_tables(token_positions, width):
    half_width = width // 2
    inverse_freq = jnp.exp(
        jnp.arange(half_width, dtype=jnp.float32) * (-2.0 / width) * math.log(rope_base)
    )
    angles = token_positions.astype(jnp.float32)[:, None] * inverse_freq[None, :]
    return jnp.cos(angles)[:, None, :], jnp.sin(angles)[:, None, :]


def head_norm_rotate(values, gain_vec, cosine, sine_part):
    mean_sq = jnp.mean(values * values, axis=-1, keepdims=True)
    values = values * lax.rsqrt(mean_sq + epsilon) * gain_vec.astype(jnp.float32)
    half_width = values.shape[-1] // 2
    front = values[..., :half_width]
    back = values[..., half_width:]
    return jnp.concatenate(
        [front * cosine - back * sine_part, back * cosine + front * sine_part], axis=-1
    )


def row_tables(lengths_row, prefix_row, page_rows, row_count):
    ends_at = jnp.cumsum(lengths_row)
    starts_at = ends_at - lengths_row
    row_ids = jnp.arange(row_count, dtype=jnp.int32)
    owners = jnp.sum((row_ids[:, None] >= ends_at[None, :]).astype(jnp.int32), axis=1)
    group_members = owners[:, None] == jnp.arange(lengths_row.shape[0], dtype=jnp.int32)[None, :]
    offsets = PAGE * prefix_row[None, :] + row_ids[:, None] - starts_at[None, :]
    token_positions = jnp.sum(jnp.where(group_members, offsets, 0), axis=1)
    page_ids = jnp.arange(page_rows.shape[1], dtype=jnp.int32)
    listed = (page_rows[:, :, None] == page_ids[None, None, :]) & (
        page_ids[None, :, None] < prefix_row[:, None, None]
    )
    page_used = jnp.sum(listed.astype(jnp.float32), axis=1)
    return (owners, group_members, token_positions, page_used)


def apply_adapter(lowrank_inner, group_members, chosen_up):
    masked = lowrank_inner[:, None, :] * group_members.astype(lowrank_inner.dtype)[:, :, None]
    return jnp.einsum("gjr,jrc->gc", masked, chosen_up, preferred_element_type=jnp.float32)


def shards(
    hidden_input,
    input_norm_gain,
    query_norm_gain,
    key_norm_gain,
    query_weight,
    key_value_weight,
    output_weight,
    adapter_down_qkv,
    adapter_down_output,
    adapter_up_query,
    adapter_up_key_value,
    adapter_up_output,
    pool,
    lengths,
    cached_prefix_pages,
    prefix_page_table,
    adapter_of_request,
    adapter_storage,
):
    mi = lax.axis_index("mlp")
    begin = mi // 2 * HEAD_SIZE
    bf16 = jnp.bfloat16
    own_wkv = lax.dynamic_slice_in_dim(key_value_weight, begin, HEAD_SIZE, 2).reshape(128, 256)
    own_ukv = lax.dynamic_slice_in_dim(adapter_up_key_value, begin, HEAD_SIZE, 3).reshape(2, 16, 256)
    cached = lax.dynamic_slice_in_dim(pool, begin, HEAD_SIZE, 2)
    gain_rows = input_norm_gain.astype(jnp.float32).reshape(16, 1, COLS)
    gain_own = lax.dynamic_slice_in_dim(gain_rows, mi, 1, 0).reshape(1, COLS)
    wo_local = jnp.transpose(output_weight, (1, 2, 0))

    smem = pl.BlockSpec(memory_space=pltpu.SMEM)
    vmem = pl.BlockSpec(memory_space=pltpu.VMEM)
    hbm = pl.BlockSpec(memory_space=pl.ANY)
    sems = 400
    hid_all, mid_all, late_all, wo_all, low = pl.pallas_call(
        gather_kernel,
        out_shape=(
            jax.ShapeDtypeStruct((16, ROWS, COLS), bf16),
            jax.ShapeDtypeStruct((32, 320, COLS), bf16),
            jax.ShapeDtypeStruct((32, 64, COLS), bf16),
            jax.ShapeDtypeStruct((16, 256, COLS), bf16),
            jax.ShapeDtypeStruct((64, ROWS), jnp.float32),
        ),
        in_specs=[smem] * 3 + [vmem] * 2 + [hbm] * 8,
        out_specs=(hbm, hbm, hbm, hbm, vmem),
        scratch_shapes=[
            pltpu.VMEM((32, 96, COLS), bf16),
            pltpu.VMEM((16, 64, ROWS), bf16),
            pltpu.SemaphoreType.DMA((sems,)),
            pltpu.SemaphoreType.DMA((sems,)),
            pltpu.SemaphoreType.DMA((16,)),
        ],
        compiler_params=pltpu.CompilerParams(collective_id=0, has_side_effects=True),
        name="gather",
    )(
        lengths,
        adapter_of_request.reshape(1, 4),
        adapter_storage,
        hidden_input,
        gain_own,
        adapter_down_qkv,
        query_weight,
        own_wkv,
        adapter_up_query,
        own_ukv,
        adapter_down_output,
        adapter_up_output,
        wo_local,
    )

    row_count = ROWS
    owners, group_members, token_positions, page_used = row_tables(
        lengths[0], cached_prefix_pages[0], prefix_page_table[0], row_count
    )
    slot_indices = jnp.take(adapter_storage, adapter_of_request[0, :, 0], axis=0)
    hid32 = hid_all.astype(jnp.float32)
    scale = lax.rsqrt(jnp.sum(hid32 * hid32, axis=(0, 2)) / 4096.0 + epsilon)[:, None]
    scaled = (hid32 * gain_rows).astype(bf16)
    weights = mid_all[:, 0:256].reshape(16, 2, 2, 128, 256)
    weights = jnp.transpose(weights, (0, 1, 3, 2, 4)).reshape(4096, 512)
    wide = jnp.transpose(scaled, (1, 0, 2)).reshape(ROWS, 4096)
    total = jnp.dot(wide, weights, preferred_element_type=jnp.float32)
    low_t = low.T.astype(bf16)
    ups_q = jnp.take(mid_all[:, 256:288].reshape(64, 16, 256), slot_indices, axis=0)
    ups_kv = jnp.take(mid_all[:, 288:320].reshape(64, 16, 256), slot_indices, axis=0)
    query_plain = (
        scale * (total[:, 0:256] + apply_adapter(low_t[:, 0:16], group_members, ups_q))
    ).astype(bf16)
    key_plain = (
        scale
        * (total[:, 256:384] + apply_adapter(low_t[:, 16:32], group_members, ups_kv[:, :, 0:128]))
    ).astype(bf16)
    value_plain = (
        scale
        * (total[:, 384:512] + apply_adapter(low_t[:, 32:48], group_members, ups_kv[:, :, 128:]))
    ).astype(bf16)
    cosine, sine_part = rotary_tables(token_positions, HEAD_SIZE)
    query_rotated = head_norm_rotate(
        query_plain.astype(jnp.float32).reshape(row_count, 2, HEAD_SIZE),
        query_norm_gain,
        cosine,
        sine_part,
    ).astype(bf16)
    key_rotated = head_norm_rotate(
        key_plain.astype(jnp.float32).reshape(row_count, 1, HEAD_SIZE),
        key_norm_gain,
        cosine,
        sine_part,
    ).astype(bf16)[:, 0]
    local_cache = jnp.stack([key_rotated, value_plain], axis=1)
    new_cache = lax.dynamic_slice_in_dim(local_cache, mi % 2 * 64, 64, 2)
    key_matrix = jnp.concatenate([cached[:, 0], key_rotated], axis=0)
    value_matrix = jnp.concatenate([cached[:, 1], value_plain], axis=0)
    pool_ok = jnp.dot(group_members.astype(jnp.float32), page_used, precision=lax.Precision.HIGHEST)
    pool_ok = jnp.repeat(pool_ok, PAGE, axis=1) > 0.5
    row_ids = jnp.arange(row_count, dtype=jnp.int32)
    causal = (owners[:, None] == owners[None, :]) & (row_ids[None, :] <= row_ids[:, None])
    allowed = jnp.concatenate([pool_ok, causal], axis=1)
    scores = jnp.einsum(
        "ghd,sd->hgs", query_rotated, key_matrix, preferred_element_type=jnp.float32
    ) / math.sqrt(HEAD_SIZE)
    exp_scores = jnp.where(allowed[None], jnp.exp(scores), 0.0)
    softmax = (exp_scores / jnp.sum(exp_scores, axis=-1, keepdims=True)).astype(bf16)
    attended = jnp.einsum("hgs,sd->ghd", softmax, value_matrix, preferred_element_type=jnp.float32)
    attended = attended.astype(bf16).reshape(row_count, COLS)
    downs = jnp.take(late_all[:, 0:32].reshape(64, 16, 256), slot_indices, axis=0)
    terms = jnp.einsum("jrc,gc->jrg", downs, attended, preferred_element_type=jnp.float32)
    low_part = jnp.sum(terms * group_members.astype(jnp.float32).T[:, None, :], axis=0)
    low_part = jnp.pad(low_part.astype(bf16), ((0, 16), (0, 0)))
    att_all, low_all = pl.pallas_call(
        gather_attended_kernel,
        out_shape=(
            jax.ShapeDtypeStruct((16, ROWS, COLS), bf16),
            jax.ShapeDtypeStruct((16, 32, ROWS), bf16),
        ),
        in_specs=[hbm] * 2,
        out_specs=(hbm, hbm),
        scratch_shapes=[
            pltpu.SemaphoreType.DMA((80,)),
            pltpu.SemaphoreType.DMA((80,)),
            pltpu.SemaphoreType.DMA((2,)),
        ],
        compiler_params=pltpu.CompilerParams(collective_id=1, has_side_effects=True),
        name="gather_attended",
    )(attended, low_part)
    ups_out = jnp.take(late_all[:, 32:64].reshape(64, 16, 256), slot_indices, axis=0)
    low_sum = jnp.sum(low_all[:, 0:16].astype(jnp.float32), axis=0).T.astype(bf16)
    update = jnp.einsum("mgk,mck->gc", att_all, wo_all, preferred_element_type=jnp.float32)
    attention_update = (update + apply_adapter(low_sum, group_members, ups_out)).astype(bf16)
    return (attention_update, new_cache)


def solution(mesh):
    return jax.shard_map(
        shards,
        mesh=mesh,
        in_specs=(
            P("req", "mlp"),
            P(),
            P(),
            P(),
            P("req", "mlp"),
            P("req", None, None),
            P("mlp", None, "req"),
            P("req", None, "mlp"),
            P("req", None, "mlp"),
            P("req", None, "mlp"),
            P("req", None, None, None),
            P("req", None, "mlp"),
            P("req", None, None),
            P("req", None),
            P("req", None),
            P("req", None, None),
            P("req", None, None),
            P(),
        ),
        out_specs=(P("req", "mlp"), P("req", None, "mlp")),
        check_vma=False,
    )
```

```python
import functools
import math

import jax
import jax.numpy as jnp
import numpy as np
from jax import lax
from jax.experimental import pallas as pl
from jax.experimental.pallas import tpu as pltpu
from jax.sharding import PartitionSpec as P

QUERY_HEADS = 32
KEY_VALUE_HEADS = 8
HEAD_SIZE = 128
ADAPTER_RANK = 16
PAGE = 64
MESH = pl.DeviceIdType.MESH

epsilon = 1e-06
rope_base = 1000000.0

Z_COUNT, NX, NY = 16, 4, 4
ROWS, COLS = 384, 256


class Links:
    def __init__(self, send, recv):
        self.send, self.recv, self.used, self.pending = send, recv, 0, []

    def start(self, src, dst, device):
        slot = self.used
        self.used += 1
        copy = pltpu.make_async_remote_copy(
            src_ref=src,
            dst_ref=dst,
            send_sem=self.send.at[slot],
            recv_sem=self.recv.at[slot],
            device_id=device,
            device_id_type=MESH,
        )
        copy.start()
        self.pending.append(copy)
        return copy

    def drain(self):
        for copy in self.pending:
            copy.wait_send()
        self.pending = []


class Place:
    def __init__(self):
        self.r = lax.axis_index("req")
        self.m = lax.axis_index("mlp")
        self.x = lax.rem(self.m, NX)
        self.y = lax.div(self.m, NX)

    def along(self, axis, step):
        if axis == "x":
            return self.m - self.x + lax.rem(self.x + (step + NX), NX)
        return lax.rem(self.m + (step + NY) * NX, NX * NY)

    def at(self, axis_a, i, axis_b, j):
        x = self.x + (i if axis_a == "x" else j) + NX
        y = self.y + (i if axis_a == "y" else j) + NY
        return lax.rem(y, NY) * NX + lax.rem(x, NX)


def barrier(place, whole_plane):
    sem = pltpu.get_barrier_semaphore()
    n = 0
    r, m = place.r, place.m
    for other in (lax.rem(r + 2, 32), lax.rem(r + 30, 32), r + 1 - 2 * lax.rem(r, 2)):
        pl.semaphore_signal(sem, inc=1, device_id=(other, m), device_id_type=MESH)
        n += 1
    for d in range(1, NX * NY):
        other = lax.rem(m + d, NX * NY)
        pl.semaphore_signal(sem, inc=1, device_id=(r, other), device_id_type=MESH)
        n += 1
    pl.semaphore_wait(sem, n)


class PlaneGather:
    def __init__(self, links, place, buf, rows):
        self.links, self.place, self.buf, self.rows = links, place, buf, rows
        self.p1, self.p2, self.q1, self.q2 = {}, {}, {}, {}
        self.axes = [("x", "y"), ("y", "x")]

    def view(self, h, piece, part=None):
        rows = self.rows // 2
        begin = h * rows
        if part is not None:
            rows //= 2
            begin += part * rows
        return self.buf.at[piece, pl.ds(begin, rows), :]

    def send(self, h, axis, step, piece, part=None):
        view = self.view(h, piece, part)
        return self.links.start(view, view, (self.place.r, self.place.along(axis, step)))

    def piece(self, h, i):
        a, b = self.axes[h]
        return self.place.at(a, i, b, 0)

    def start_second(self, h, i):
        b = self.axes[h][1]
        for s in (1, -1):
            self.q1[h, i, s] = self.send(h, b, s, self.piece(h, i))

    def e0(self):
        for h in range(2):
            a = self.axes[h][0]
            for s in (1, -1):
                self.p1[h, s] = self.send(h, a, s, self.place.m)
        for h in range(2):
            self.start_second(h, 0)

    def e1(self):
        for h in range(2):
            a = self.axes[h][0]
            for s in (1, -1):
                self.p1[h, s].wait_recv()
                self.p2[h, s] = self.send(h, a, s, self.piece(h, -s), 0 if s == 1 else 1)
        for h in range(2):
            for s in (1, -1):
                self.start_second(h, -s)

    def e2(self):
        for h in range(2):
            for s in (1, -1):
                self.p2[h, s].wait_recv()
            self.start_second(h, 2)

    def e3(self, i):
        for h in range(2):
            a, b = self.axes[h]
            for s in (1, -1):
                self.q1[h, i, s].wait_recv()
                piece = self.place.at(a, i, b, -s)
                self.q2[h, i, s] = self.send(h, b, s, piece, 0 if s == 1 else 1)

    def e4(self):
        for copy in self.q2.values():
            copy.wait_recv()

    def run(self):
        self.e0()
        self.e1()
        self.e2()
        for i in (0, -1, 1, 2):
            self.e3(i)
        self.e4()


class RingGather:
    def __init__(self, links, place, view, halves):
        self.links, self.place, self.view, self.halves = links, place, view, halves
        self.z, self.sib = {}, {}

    def shard(self, t):
        return lax.rem(self.place.r + (2 * t + 32), 32)

    def send(self, t, s):
        shard = self.shard(-s * t)
        target = (lax.rem(self.place.r + (2 * s + 32), 32), self.place.m)
        if t == Z_COUNT // 2 - 1:
            view = self.halves(shard, 0 if s == 1 else 1)
        else:
            view = self.view(shard)
        self.z[t, s] = self.links.start(view, view, target)

    def sibling(self, t):
        view = self.view(self.shard(t))
        r = self.place.r
        self.sib[t] = self.links.start(view, view, (r + 1 - 2 * lax.rem(r, 2), self.place.m))

    def step(self, t):
        last = Z_COUNT // 2
        if t == 0:
            for s in (1, -1):
                self.send(0, s)
            self.sibling(0)
            return
        for s in (1, -1):
            self.z[t - 1, s].wait_recv()
            if t < last:
                self.send(t, s)
        if t < last:
            for s in (1, -1):
                self.sibling(-s * t)
        else:
            self.sibling(last)

    def siblings(self, t):
        for i in {t, -t} if t < Z_COUNT // 2 else {t}:
            self.sib[i].wait_recv()

    def finish(self):
        for copy in self.sib.values():
            copy.wait_recv()


class Fused:
    def __init__(self, ins, outs, scratch):
        (
            self.lengths,
            self.prefix,
            self.pages,
            self.chosen,
            self.storage,
            self.hid,
            self.gain,
            self.head_gain,
            self.freq,
            self.down_qkv,
            self.wq,
            self.wkv,
            self.up_q,
            self.up_kv,
            self.down_out,
            self.up_out,
            self.wo,
            self.pool,
        ) = ins
        self.out, self.cache = outs
        (
            self.hid_all,
            self.scaled,
            self.down_all,
            self.mid_all,
            self.late_all,
            self.wo_all,
            self.low_all,
            self.att_all,
            self.low_out_all,
            self.cached,
            self.acc,
            self.sq,
            self.cos,
            self.sin,
            self.query,
            self.key,
            self.turned,
            self.pool_ok,
            send,
            recv,
            self.local,
        ) = scratch
        self.place = Place()
        self.r, self.m = self.place.r, self.place.m
        self.chip = lax.div(self.r, 2)
        self.links = Links(send, recv)
        links, place = self.links, self.place
        self.plane = PlaneGather(links, place, self.hid_all, ROWS)
        self.lows = PlaneGather(links, place, self.low_all, 64)
        self.att = PlaneGather(links, place, self.att_all, ROWS)
        self.low_outs = PlaneGather(links, place, self.low_out_all, 32)
        self.early = RingGather(links, place, *rows_of(self.down_all, 0, 96))
        self.mid = [
            RingGather(links, place, *rows_of(self.mid_all, begin, rows))
            for begin, rows in MID_PARTS
        ]
        self.late = RingGather(links, place, *rows_of(self.late_all, 0, 64))
        self.wide = RingGather(
            links,
            place,
            lambda shard: self.wo_all.at[:, pl.ds(shard * 8, 8), :],
            lambda shard, part: self.wo_all.at[pl.ds(8 * part, 8), pl.ds(shard * 8, 8), :],
        )


    def stage(self):
        r, m = self.r, self.m
        staged = []

        def move(src, dst):
            copy = pltpu.make_async_copy(src, dst, self.local.at[len(staged)])
            copy.start()
            staged.append(copy)

        for i in range(2):
            move(self.down_qkv.at[i], self.down_all.at[r, pl.ds(48 * i, 48), :])
        move(self.hid, self.hid_all.at[m])
        move(self.wq, self.mid_all.at[r, pl.ds(0, 128), :])
        move(self.wkv, self.mid_all.at[r, pl.ds(128, 128), :])
        for i in range(2):
            move(self.up_q.at[i], self.mid_all.at[r, pl.ds(256 + 16 * i, 16), :])
            move(self.up_kv.at[i], self.mid_all.at[r, pl.ds(288 + 16 * i, 16), :])
            move(self.down_out.at[i], self.late_all.at[r, pl.ds(16 * i, 16), :])
            move(self.up_out.at[i], self.late_all.at[r, pl.ds(32 + 16 * i, 16), :])
        move(self.wo.at[m], self.wo_all.at[m, pl.ds(r * 8, 8), :])
        move(self.pool, self.cached)
        return staged

    def swap(self):
        self.swaps = []
        for d in range(1, NX * NY):
            other = lax.rem(self.m + d, NX * NY)
            self.swaps.append(
                self.links.start(
                    self.wo.at[other],
                    self.wo_all.at[self.m, pl.ds(self.r * 8, 8), :],
                    (self.r, other),
                )
            )

    def ends(self):
        e1 = self.lengths[0, 0]
        e2 = e1 + self.lengths[0, 1]
        e3 = e2 + self.lengths[0, 2]
        return e1, e2, e3

    def owner(self, index):
        e1, e2, e3 = self.ends()
        return (
            (index >= e1).astype(jnp.int32)
            + (index >= e2).astype(jnp.int32)
            + (index >= e3).astype(jnp.int32)
        )

    def owner_lane(self):
        return self.owner(lax.broadcasted_iota(jnp.int32, (1, ROWS), 1))

    def owner_row(self, lanes):
        return self.owner(lax.broadcasted_iota(jnp.int32, (ROWS, lanes), 0))

    def tables(self):
        e1, e2, e3 = self.ends()
        row = lax.broadcasted_iota(jnp.int32, (ROWS, HEAD_SIZE), 0)
        owner = self.owner(row)
        shift = PAGE * self.prefix[0, 0] + jnp.zeros_like(row)
        for j, begin in ((1, e1), (2, e2), (3, e3)):
            shift = jnp.where(owner == j, PAGE * self.prefix[0, j] - begin, shift)
        angles = (row + shift).astype(jnp.float32) * self.freq[...]
        self.cos[...] = jnp.cos(angles)
        lane = lax.broadcasted_iota(jnp.int32, (ROWS, HEAD_SIZE), 1)
        sine = jnp.sin(angles)
        self.sin[...] = jnp.where(lane < HEAD_SIZE // 2, -sine, sine)

    def pool_mask(self):
        page = lax.div(lax.broadcasted_iota(jnp.int32, (1, 8 * PAGE), 1), PAGE)
        owner = self.owner_row(8 * PAGE)
        mask = jnp.zeros((ROWS, 8 * PAGE), jnp.float32)
        for j in range(4):
            used = jnp.zeros((1, 8 * PAGE), jnp.float32)
            count = self.prefix[0, j]
            for i in range(8):
                wanted = self.pages[j, i] + 64 * jnp.maximum(i + 1 - count, 0)
                used = jnp.where(page == wanted, 1.0, used)
            mask = jnp.where(owner == j, used, mask)
        self.pool_ok[...] = mask


    def slot(self, j):
        return self.storage[self.chosen[0, j]]

    def rows_at(self, ref, begin, rows, j):
        slot = self.slot(j)
        return ref[slot // 2, pl.ds(begin + (slot % 2) * rows, rows), :]

    def own_terms(self):
        scaled = (self.hid[...].astype(jnp.float32) * self.gain[pl.ds(self.m, 1), :]).astype(
            jnp.bfloat16
        )
        owner = self.owner_lane()
        low = jnp.zeros((48, ROWS), jnp.float32)
        for j in range(4):
            slot = self.slot(j)
            down = self.down_all[slot // 2, pl.ds((slot % 2) * 48, 48), :]
            terms = lax.dot_general(
                down, scaled, (((1,), (1,)), ((), ())), preferred_element_type=jnp.float32
            )
            low = low + jnp.where(owner == j, terms, 0.0)
        self.low_all[self.m, 0:48, :] = low.astype(jnp.bfloat16)
        self.low_all[self.m, 48:64, :] = jnp.zeros((16, ROWS), jnp.bfloat16)

    def scale_piece(self, i):
        h = self.hid_all[i].astype(jnp.float32)
        self.sq[...] += h * h
        self.scaled[i] = (h * self.gain[pl.ds(i, 1), :]).astype(jnp.bfloat16)

    def scale_all(self):
        self.sq[...] = jnp.zeros_like(self.sq)
        self.acc[...] = jnp.zeros_like(self.acc)

        def one(i, carry):
            self.scale_piece(i)
            return carry

        lax.fori_loop(0, 16, one, 0)

    def project(self, chip):
        x = self.scaled[chip]
        for part in range(2):
            w = jnp.concatenate(
                [
                    self.mid_all[2 * chip, pl.ds(128 * part, 128), :],
                    self.mid_all[2 * chip + 1, pl.ds(128 * part, 128), :],
                ],
                axis=0,
            )
            self.acc[part] += jnp.dot(x, w, preferred_element_type=jnp.float32)

    def project_step(self, t):
        chips = [self.chip] if t == 0 else [lax.rem(self.chip + t, 16)]
        if 0 < t < 8:
            chips.append(lax.rem(self.chip + 16 - t, 16))
        for chip in chips:
            self.project(chip)

    def masked_terms(self, low):
        owner = self.owner_lane()
        return jnp.concatenate([jnp.where(owner == j, low, 0.0) for j in range(4)], axis=0)

    def ups(self, ref, begin):
        return jnp.concatenate([self.rows_at(ref, begin, 16, j) for j in range(4)], axis=0)

    def head(self, values, gain_row):
        values = values.astype(jnp.bfloat16).astype(jnp.float32)
        mean_sq = jnp.mean(values * values, axis=-1, keepdims=True)
        values = values * lax.rsqrt(mean_sq + epsilon) * self.head_gain[gain_row : gain_row + 1, :]
        turned = pltpu.roll(values, HEAD_SIZE // 2, 1)
        return values * self.cos[...] + turned * self.sin[...]

    def finish_projection(self):
        low = jnp.zeros((48, ROWS), jnp.float32)
        for i in range(16):
            low = low + self.low_all[i, 0:48, :].astype(jnp.float32)
        up_q = self.ups(self.mid_all, 256)
        up_kv = self.ups(self.mid_all, 288)
        q_terms = self.masked_terms(low[0:16]).T.astype(jnp.bfloat16)
        k_terms = self.masked_terms(low[16:32]).T.astype(jnp.bfloat16)
        v_terms = self.masked_terms(low[32:48]).T.astype(jnp.bfloat16)
        scale = lax.rsqrt(jnp.sum(self.sq[...], axis=1, keepdims=True) / 4096.0 + epsilon)
        dot = functools.partial(jnp.dot, preferred_element_type=jnp.float32)
        query = scale * (self.acc[0] + dot(q_terms, up_q))
        key = scale * (self.acc[1, :, 0:128] + dot(k_terms, up_kv[:, 0:128]))
        value = scale * (self.acc[1, :, 128:256] + dot(v_terms, up_kv[:, 128:256]))
        for h in range(2):
            self.query[h] = self.head(query[:, 128 * h : 128 * h + 128], 0).astype(jnp.bfloat16)
        key = self.head(key, 1)
        value = value.astype(jnp.bfloat16)
        self.key[0] = key.astype(jnp.bfloat16)
        self.key[1] = value
        self.turned[0] = key.T
        self.turned[1] = value.astype(jnp.float32).T

    def store_cache(self):
        first = pl.multiple_of(lax.rem(self.m, 2) * 64, 64)
        for i in range(2):
            self.cache[i] = self.turned[i, pl.ds(first, 64), :].astype(jnp.bfloat16)

    def attend(self, h):
        query = self.query[h]
        nt = (((1,), (1,)), ((), ()))
        by = 1.0 / math.sqrt(HEAD_SIZE)

        def parts(keys, mask):
            scores = lax.dot_general(query, keys, nt, preferred_element_type=jnp.float32)
            return jnp.where(mask, jnp.exp(scores * by - 4.0), 0.0)

        old = parts(self.cached[:, 0:128], self.pool_ok[...] > 0.5)
        row = lax.broadcasted_iota(jnp.int32, (ROWS, ROWS), 0)
        lane = lax.broadcasted_iota(jnp.int32, (ROWS, ROWS), 1)
        seen = (self.owner(row) == self.owner_lane()) & (lane <= row)
        new = parts(self.key[0], seen)
        total = jnp.sum(old, axis=1, keepdims=True) + jnp.sum(new, axis=1, keepdims=True)
        values = jnp.dot(
            old.astype(jnp.bfloat16), self.cached[:, 128:256], preferred_element_type=jnp.float32
        ) + jnp.dot(new.astype(jnp.bfloat16), self.key[1], preferred_element_type=jnp.float32)
        self.att_all[self.m, :, 128 * h : 128 * h + 128] = (values / total).astype(jnp.bfloat16)

    def own_output_terms(self):
        downs = self.ups(self.late_all, 0)
        terms = lax.dot_general(
            downs,
            self.att_all[self.m],
            (((1,), (1,)), ((), ())),
            preferred_element_type=jnp.float32,
        )
        owner = self.owner_lane()
        low = jnp.zeros((16, ROWS), jnp.float32)
        for j in range(4):
            low = low + jnp.where(owner == j, terms[16 * j : 16 * j + 16], 0.0)
        self.low_out_all[self.m, 0:16, :] = low.astype(jnp.bfloat16)
        self.low_out_all[self.m, 16:32, :] = jnp.zeros((16, ROWS), jnp.bfloat16)

    def output_piece(self, piece, first=False):
        update = lax.dot_general(
            self.att_all[piece],
            self.wo_all[piece],
            (((1,), (1,)), ((), ())),
            preferred_element_type=jnp.float32,
        )
        if first:
            self.acc[0] = update
        else:
            self.acc[0] += update

    def finish_output(self):
        low = jnp.zeros((16, ROWS), jnp.float32)
        for i in range(16):
            low = low + self.low_out_all[i, 0:16, :].astype(jnp.float32)
        terms = self.masked_terms(low).T.astype(jnp.bfloat16)
        update = jnp.dot(terms, self.ups(self.late_all, 32), preferred_element_type=jnp.float32)
        self.out[...] = (self.acc[0] + update).astype(jnp.bfloat16)

    def late_step(self, t):
        self.late.step(t)
        self.wide.step(t)

    def mid_step(self, t):
        for ring in self.mid:
            ring.step(t)

    def mid_siblings(self, t):
        for ring in self.mid:
            ring.siblings(t)


def rows_of(ref, begin, rows):
    return (
        lambda shard: ref.at[shard, pl.ds(begin, rows), :],
        lambda shard, part: ref.at[shard, pl.ds(begin + part * (rows // 2), rows // 2), :],
    )


MID_PARTS = ((0, 160), (160, 160))


def layer_kernel(*refs):
    f = Fused(refs[:18], refs[18:20], refs[20:])
    staged = f.stage()
    barrier(f.place, True)
    for copy in staged:
        copy.wait()

    f.early.step(0)
    f.plane.e0()
    f.mid_step(0)
    f.swap()
    f.tables()
    f.early.step(1)
    f.plane.e1()
    f.mid_step(1)
    f.pool_mask()
    f.early.step(2)
    f.plane.e2()
    f.mid_step(2)
    f.early.step(3)
    f.plane.e3(0)
    f.mid_step(3)
    f.early.step(4)
    f.plane.e3(-1)
    f.plane.e3(1)
    f.mid_step(4)
    for copy in f.swaps:
        copy.wait_recv()
    f.late_step(0)
    f.early.step(5)
    f.plane.e3(2)
    f.mid_step(5)
    f.early.step(6)
    f.plane.e4()
    f.mid_step(6)
    f.scale_all()
    f.early.step(7)
    f.mid_step(7)
    f.late_step(1)
    f.early.step(8)
    f.early.finish()
    f.own_terms()
    f.lows.e0()
    for t in range(4):
        f.mid_siblings(t)
        f.project_step(t)
    f.lows.e1()
    f.mid_step(8)
    f.late_step(2)
    f.lows.e2()
    for t in range(4, 7):
        f.mid_siblings(t)
        f.project_step(t)
    for i in (0, -1, 1, 2):
        f.lows.e3(i)
    f.late_step(3)
    for t in range(7, 9):
        f.mid_siblings(t)
        f.project_step(t)
    f.lows.e4()
    f.finish_projection()
    f.late_step(4)
    f.attend(0)
    f.late_step(5)
    f.attend(1)
    f.att.e0()
    f.late_step(6)
    f.store_cache()
    f.att.e1()
    f.late_step(7)
    f.att.e2()
    f.late_step(8)
    f.late.finish()
    f.wide.finish()
    f.own_output_terms()
    f.low_outs.e0()
    f.output_piece(f.m, True)
    f.att.e3(0)
    f.att.e3(-1)
    f.low_outs.e1()
    f.att.e3(1)
    f.low_outs.e2()
    f.att.e3(2)
    for i in (0, -1, 1, 2):
        f.low_outs.e3(i)
    f.att.e4()
    for d in range(1, 16):
        f.output_piece(lax.rem(f.m + d, 16))
    f.low_outs.e4()
    f.finish_output()
    f.links.drain()


def shards(
    hidden_input,
    input_norm_gain,
    query_norm_gain,
    key_norm_gain,
    query_weight,
    key_value_weight,
    output_weight,
    adapter_down_qkv,
    adapter_down_output,
    adapter_up_query,
    adapter_up_key_value,
    adapter_up_output,
    pool,
    lengths,
    cached_prefix_pages,
    prefix_page_table,
    adapter_of_request,
    adapter_storage,
):
    mi = lax.axis_index("mlp")
    begin = mi // 2 * HEAD_SIZE
    bf16, f32 = jnp.bfloat16, jnp.float32
    own_wkv = lax.dynamic_slice_in_dim(key_value_weight, begin, HEAD_SIZE, 2).reshape(128, 256)
    own_ukv = lax.dynamic_slice_in_dim(adapter_up_key_value, begin, HEAD_SIZE, 3).reshape(2, 16, 256)
    cached = lax.dynamic_slice_in_dim(pool, begin, HEAD_SIZE, 2).reshape(512, 256)
    half = HEAD_SIZE // 2
    freq = np.exp(
        np.arange(half, dtype=np.float32) * np.float32(-2.0 / HEAD_SIZE) * np.float32(math.log(rope_base))
    ).astype(np.float32)
    freq = np.concatenate([freq, freq])[None, :]

    smem = pl.BlockSpec(memory_space=pltpu.SMEM)
    vmem = pl.BlockSpec(memory_space=pltpu.VMEM)
    hbm = pl.BlockSpec(memory_space=pl.ANY)
    sems = 360
    update, cache = pl.pallas_call(
        layer_kernel,
        out_shape=(
            jax.ShapeDtypeStruct((ROWS, COLS), bf16),
            jax.ShapeDtypeStruct((2, 64, ROWS), bf16),
        ),
        in_specs=[smem] * 5 + [vmem] * 4 + [hbm] * 9,
        out_specs=(vmem, vmem),
        scratch_shapes=[
            pltpu.VMEM((16, ROWS, COLS), bf16),
            pltpu.VMEM((16, ROWS, COLS), bf16),
            pltpu.VMEM((32, 96, COLS), bf16),
            pltpu.VMEM((32, 320, COLS), bf16),
            pltpu.VMEM((32, 64, COLS), bf16),
            pltpu.VMEM((16, 256, COLS), bf16),
            pltpu.VMEM((16, 64, ROWS), bf16),
            pltpu.VMEM((16, ROWS, COLS), bf16),
            pltpu.VMEM((16, 32, ROWS), bf16),
            pltpu.VMEM((512, COLS), bf16),
            pltpu.VMEM((2, ROWS, COLS), f32),
            pltpu.VMEM((ROWS, COLS), f32),
            pltpu.VMEM((ROWS, HEAD_SIZE), f32),
            pltpu.VMEM((ROWS, HEAD_SIZE), f32),
            pltpu.VMEM((2, ROWS, HEAD_SIZE), bf16),
            pltpu.VMEM((2, ROWS, HEAD_SIZE), bf16),
            pltpu.VMEM((2, HEAD_SIZE, ROWS), f32),
            pltpu.VMEM((ROWS, 8 * PAGE), f32),
            pltpu.SemaphoreType.DMA((sems,)),
            pltpu.SemaphoreType.DMA((sems,)),
            pltpu.SemaphoreType.DMA((16,)),
        ],
        compiler_params=pltpu.CompilerParams(
            collective_id=0, has_side_effects=True, vmem_limit_bytes=56 * 2**20
        ),
        name="layer",
    )(
        lengths,
        cached_prefix_pages,
        prefix_page_table.reshape(4, 8),
        adapter_of_request.reshape(1, 4),
        adapter_storage,
        hidden_input,
        input_norm_gain.astype(f32).reshape(16, COLS),
        jnp.stack([query_norm_gain, key_norm_gain]).astype(f32),
        freq,
        adapter_down_qkv,
        query_weight,
        own_wkv,
        adapter_up_query,
        own_ukv,
        adapter_down_output,
        adapter_up_output,
        jnp.transpose(output_weight, (1, 2, 0)),
        cached,
    )
    return (update, jnp.transpose(cache, (2, 0, 1)))


def solution(mesh):
    return jax.shard_map(
        shards,
        mesh=mesh,
        in_specs=(
            P("req", "mlp"),
            P(),
            P(),
            P(),
            P("req", "mlp"),
            P("req", None, None),
            P("mlp", None, "req"),
            P("req", None, "mlp"),
            P("req", None, "mlp"),
            P("req", None, "mlp"),
            P("req", None, None, None),
            P("req", None, "mlp"),
            P("req", None, None),
            P("req", None),
            P("req", None),
            P("req", None, None),
            P("req", None, None),
            P(),
        ),
        out_specs=(P("req", "mlp"), P("req", None, "mlp")),
        check_vma=False,
    )
```
